256 devices in a mesh: grid: 8 (over y, core), wide: 32 (over z, x).
Axes of the slice: x: 4, y: 4, z: 8, core: 2. Of those that a mesh axis runs over, the one named last changes fastest.
Arguments:
- values: bfloat16 [3584, 64, 4096], P(('grid', 'wide')), may hold values from 0 to 1
- a_block: int32 [3584], P(('grid', 'wide')), may hold values from 0 to 63, as said below
- b_block: int32 [3584], P(('grid', 'wide')), may hold values from 0 to 15
- c_block: int32 [3584], P(('grid', 'wide')), may hold values from 0 to 63
- held: int32 [3584], P(('grid', 'wide')), may hold values from 0 to 1, as said below
- factor_a: bfloat16 [32768, 256], P(('grid', 'wide')), may hold values from -6 to 6
- factor_b: bfloat16 [32768, 256], P(('wide', 'grid')), may hold values from -2.390625 to 2.390625
- factor_c: bfloat16 [4096, 256], replicated, may hold values from -2.390625 to 2.390625
Outputs:
- next_a: float32 [32768, 256], P(('grid', 'wide'))
- next_b: float32 [32768, 256], P(('wide', 'grid'))
- held_loss: float32 [], replicated
The draws below stay inside these ranges and needn't reach their ends.
Inputs may be any that keep to these rules, and one draw needn't show every extreme that they name: Among the blocks of one device, at most 1 have a_block values with the same a_block // 2; on some device some such value is shared by exactly 1 block. Every device holds 1 to 3 held-out blocks; some device holds exactly 3.
All inputs are finite; a program needn't handle non-finite values.
Results may differ from the reference program's by a relative error of at most 0.0011.
Values may be sent and summed in bfloat16 or wider, within the bound.
No kernel may reach another device: no remote copies, remote signals or barrier semaphores. Data moves between devices by JAX's collectives and lax.ppermute only.
A program may use at most 64 MiB of HBM per device.

```python
import jax
import jax.numpy as jnp
from jax import lax

R = 256
BS = 64
NB_DEV = 14
A_ROWS_DEV = 128
K = 4096
HELD_MAX = 3
BLOCKS = 3584
I_ROWS = 32768
J_ROWS = 32768
A_PBLK = 64
B_PBLK = 16
CAP = 1
N_WIDE = 32


def draw_a_block(key, part):
    devices = BLOCKS // NB_DEV
    per_holder = A_ROWS_DEV // BS
    keys = jax.random.split(key, devices)

    def single(sub_key):
        first_key, second_key = jax.random.split(sub_key)
        pool = jnp.arange(CAP * N_WIDE, dtype=jnp.int32) % N_WIDE
        holders = jax.random.permutation(first_key, pool)[:NB_DEV]
        within = jax.random.randint(second_key, (NB_DEV,), 0, per_holder, dtype=jnp.int32)
        return (holders, within)
    holders, within = jax.vmap(single)(keys)
    shifted = (holders[0] - holders[0, 0] + N_WIDE - 1) % N_WIDE
    holders = holders.at[0].set(shifted)
    within = within.at[0, 0].set(per_holder - 1)
    return (holders * per_holder + within).reshape(-1).astype(jnp.int32)


def draw_held(key, part):
    devices = BLOCKS // NB_DEV
    count_key, order_key = jax.random.split(jax.random.fold_in(key, 7))
    counts = jax.random.randint(count_key, (devices,), 1, HELD_MAX + 1, dtype=jnp.int32)
    counts = counts.at[0].set(HELD_MAX)
    orders = jax.vmap(lambda sub_key: jax.random.permutation(sub_key, NB_DEV))(jax.random.split(order_key, devices))
    return (orders < counts[:, None]).astype(jnp.int32).reshape(-1)


def draw_factor_a(key, part):
    sub_key = jax.random.fold_in(key, 11)
    fraction = jnp.arange(I_ROWS, dtype=jnp.float32) / (I_ROWS - 1.0)
    spread = 0.12 * jnp.exp(fraction * jnp.log(20.0))
    noise = jnp.clip(jax.random.normal(sub_key, (I_ROWS, R), jnp.float32), -2.4, 2.4)
    return (noise * spread[:, None]).astype(jnp.bfloat16)


def plant(result, own_key, low, largest):
    longest = result.shape.index(max(result.shape))
    spots = []
    for shift in (0, 1):
        where = [jax.random.randint(jax.random.fold_in(own_key, axis), (), 0, length) for axis, length in enumerate(result.shape)]
        where[longest] = (where[longest] + shift) % result.shape[longest]
        spots.append(tuple(where))
    return result.at[spots[0]].set(low).at[spots[1]].set(largest)


def block_scale(rng, extent, pieces, smallest, largest):
    level, own = 1.0, jax.random.fold_in(rng, 6)
    for position, blocks in pieces:
        steps = jnp.exp(jax.random.uniform(jax.random.fold_in(own, position), (blocks,), jnp.float32, smallest / len(pieces), largest / len(pieces)))
        level = level * jnp.repeat(steps, extent[position] // blocks).reshape([-1 if axis == position else 1 for axis in range(len(extent))])
    return level


def gaussian(stream_key, extent, scale, limit, cuts=(), kind=jnp.bfloat16):
    factor_of = block_scale(stream_key, extent, cuts, -0.22, 0.18) if cuts else 1.0
    values = jax.random.normal(stream_key, extent, jnp.float32) * scale * factor_of
    return jnp.minimum(jnp.maximum(values, -limit), limit).astype(kind)


def setup_inputs(seed: int = 0) -> dict:
    key_of = jax.random.split(jax.random.key(seed), 9)
    values = jnp.clip(1.0 * jax.random.uniform(key_of[0], (BLOCKS, BS, BS * BS), jnp.float32) ** block_scale(key_of[0], (BLOCKS, BS, BS * BS), ((0, 256),), -0.2, 0.2), 0.0, 1.0).astype(jnp.bfloat16)
    a_block = draw_a_block(jax.random.fold_in(key_of[8], 71), 0)
    b_block = plant(jax.random.randint(key_of[2], (BLOCKS,), 0, B_PBLK), jax.random.fold_in(key_of[2], 1), 0, B_PBLK - 1).astype(jnp.int32)
    c_block = plant(jax.random.randint(key_of[3], (BLOCKS,), 0, K // BS), jax.random.fold_in(key_of[3], 1), 0, (K // BS) - 1).astype(jnp.int32)
    held = draw_held(jax.random.fold_in(key_of[8], 71), 0)
    factor_a = draw_factor_a(jax.random.fold_in(key_of[8], 71), 0)
    factor_b = gaussian(key_of[6], (J_ROWS, R), 0.4, 2.390625, ((0, 256),))
    factor_c = gaussian(key_of[7], (K, R), 0.4, 2.390625)
    return {"values": values, "a_block": a_block, "b_block": b_block, "c_block": c_block, "held": held, "factor_a": factor_a, "factor_b": factor_b, "factor_c": factor_c}


step_size = 0.05


def reference(values, a_block, b_block, c_block, held, factor_a, factor_b, factor_c):
    devices = BLOCKS // NB_DEV
    a_blocks = factor_a.reshape(I_ROWS // BS, BS, R)
    b_blocks = factor_b.reshape(J_ROWS // BS, BS, R)
    c_blocks = factor_c.reshape(K // BS, BS, R)
    highest = lax.Precision.HIGHEST

    def visit(carry, device):
        grad_a, grad_b, loss_total, held_total = carry
        start = device * NB_DEV
        entries = lax.dynamic_slice_in_dim(values, start, NB_DEV, 0).astype(jnp.float32)
        a_index = (device // N_WIDE) * A_PBLK + lax.dynamic_slice_in_dim(a_block, start, NB_DEV, 0)
        b_index = (device % N_WIDE) * B_PBLK + lax.dynamic_slice_in_dim(b_block, start, NB_DEV, 0)
        c_index = lax.dynamic_slice_in_dim(c_block, start, NB_DEV, 0)
        flags = lax.dynamic_slice_in_dim(held, start, NB_DEV, 0).astype(jnp.float32)
        a_rows = a_blocks[a_index].astype(jnp.float32)
        b_rows = b_blocks[b_index].astype(jnp.float32)
        c_rows = c_blocks[c_index].astype(jnp.float32)
        khatri = (b_rows[:, :, None, :] * c_rows[:, None, :, :]).astype(jnp.bfloat16)
        khatri = lax.optimization_barrier(khatri).astype(jnp.float32).reshape(NB_DEV, BS * BS, R)
        model = jnp.einsum("nar,nkr->nak", a_rows, khatri, precision=highest)
        weight = flags[:, None, None]
        resid = ((jax.nn.sigmoid(model) - entries) * (1.0 - weight)).astype(jnp.bfloat16)
        resid = lax.optimization_barrier(resid).astype(jnp.float32)
        loss_total = loss_total + jnp.sum((jax.nn.softplus(model) - entries * model) * weight)
        grad_rows = jnp.einsum("nak,nkr->nar", resid, khatri, precision=highest)
        partial_sum = jnp.einsum("nak,nar->nkr", resid, a_rows, precision=highest).reshape(NB_DEV, BS, BS, R)
        grad_cols = jnp.sum(partial_sum * c_rows[:, None, :, :], axis=2)
        grad_a = grad_a.at[a_index].add(grad_rows)
        grad_b = grad_b.at[b_index].add(grad_cols)
        return (grad_a, grad_b, loss_total, held_total + jnp.sum(flags)), None

    start_carry = (jnp.zeros((I_ROWS // BS, BS, R), jnp.float32), jnp.zeros((J_ROWS // BS, BS, R), jnp.float32),
                   jnp.zeros((), jnp.float32), jnp.zeros((), jnp.float32))
    final, unused = lax.scan(visit, start_carry, jnp.arange(devices, dtype=jnp.int32))
    grad_a, grad_b, loss_total, held_total = final
    next_a = factor_a.astype(jnp.float32) - step_size * grad_a.reshape(I_ROWS, R)
    next_b = factor_b.astype(jnp.float32) - step_size * grad_b.reshape(J_ROWS, R)
    held_loss = loss_total / (held_total * (BS * BS * BS))
    return next_a, next_b, held_loss
```

```python
import jax
import jax.numpy as jnp
from jax import lax
from jax.experimental import pallas as pl
from jax.experimental.pallas import tpu as pltpu
from jax.sharding import PartitionSpec as P

step_size = 0.05
chunk_rows = 8


def block_kernel(slot_at, b_at, c_at, held, values, a_rows, b_rows, c_rows, out_a, out_b):
    step = pl.program_id(0)
    side = a_rows.shape[1]
    width = a_rows.shape[2]
    span = chunk_rows * side
    pair = out_b.shape[1] - 8
    a = a_rows[0]
    c_wide = c_rows[0].astype(jnp.float32)

    @pl.when(step == 0)
    def _():
        out_a[...] = jnp.zeros_like(out_a)
        out_b[...] = jnp.zeros_like(out_b)

    def chunk(i):
        b = b_rows[0, pl.ds(i * chunk_rows, chunk_rows), :].astype(jnp.float32)
        khatri = (b[:, None, :] * c_wide[None, :, :]).astype(jnp.bfloat16).reshape(span, width)
        model = lax.dot_general(
            a, khatri, (((1,), (1,)), ((), ())), preferred_element_type=jnp.float32
        )
        return khatri, model, values[0, :, pl.ds(i * span, span)].astype(jnp.float32)

    @pl.when(held[step] == 1)
    def _():
        total = jnp.zeros((8, 128), jnp.float32)
        for i in range(side // chunk_rows):
            khatri, model, entry = chunk(i)
            soft = jnp.maximum(model, 0.0) + jnp.log1p(jnp.exp(-jnp.abs(model)))
            part = jnp.sum((soft - entry * model).reshape(side // 8, 8, span), axis=0)
            for j in range(span // 128):
                total = total + part[:, j * 128 : (j + 1) * 128]
        for g in range(out_b.shape[0]):
            out_b[g, pair:, 0:128] += total
            out_b[g, pair:, 128:256] += jnp.full((8, 128), 1.0 / 1024.0, jnp.float32)

    @pl.when(held[step] == 0)
    def _():
        acc = jnp.zeros((side, width), jnp.float32)
        where_b = b_at[step]
        group = where_b // 2
        base = (where_b % 2) * side
        for i in range(side // chunk_rows):
            khatri, model, entry = chunk(i)
            resid = (jax.nn.sigmoid(model) - entry).astype(jnp.bfloat16)
            acc = acc + jnp.dot(resid, khatri, preferred_element_type=jnp.float32)
            part = lax.dot_general(
                resid, a, (((0,), (0,)), ((), ())), preferred_element_type=jnp.float32
            )
            cols = jnp.sum(part.reshape(chunk_rows, side, width) * c_wide[None, :, :], axis=1)
            spot = pl.multiple_of(base + i * chunk_rows, 8)
            out_b[group, pl.ds(spot, chunk_rows), :] += cols
        out_a[slot_at[step]] = acc


def per_device(values, a_block, b_block, c_block, held, factor_a, factor_b, factor_c):
    blocks, side, entries = values.shape
    width = factor_a.shape[1]
    wide_count = lax.axis_size("wide")
    grid_count = lax.axis_size("grid")
    b_panel = lax.all_gather(factor_b, "grid", axis=0, tiled=True).reshape(-1, side, width)
    slot = a_block // 2
    within = a_block % 2
    matches = slot[None, :] == jnp.arange(wide_count, dtype=jnp.int32)[:, None]
    wanted = jnp.sum(jnp.where(matches, within[None, :], 0), axis=1)
    asked = lax.all_to_all(
        jnp.broadcast_to(wanted[:, None, None], (wide_count, 1, 128)), "wide", 0, 0
    )[:, 0, 0]
    second = (asked == 1)[:, None, None]
    own_a = factor_a.reshape(2, side, width)
    a_slots = lax.all_to_all(
        jnp.where(second, own_a[1][None], own_a[0][None]), "wide", 0, 0
    )
    pick = lambda array_of: pl.BlockSpec((1, side, width), array_of)
    out_a, out_b = pl.pallas_call(
        block_kernel,
        grid_spec=pltpu.PrefetchScalarGridSpec(
            num_scalar_prefetch=4,
            grid=(blocks,),
            in_specs=[
                pl.BlockSpec((1, side, entries), lambda i, s, b, c, h: (i, 0, 0)),
                pick(lambda i, s, b, c, h: (s[i], 0, 0)),
                pick(lambda i, s, b, c, h: (b[i], 0, 0)),
                pick(lambda i, s, b, c, h: (c[i], 0, 0)),
            ],
            out_specs=[
                pl.BlockSpec((wide_count, side, width), lambda i, s, b, c, h: (0, 0, 0)),
                pl.BlockSpec((grid_count, 2 * side + 8, width), lambda i, s, b, c, h: (0, 0, 0)),
            ],
        ),
        out_shape=[
            jax.ShapeDtypeStruct((wide_count, side, width), jnp.float32),
            jax.ShapeDtypeStruct((grid_count, 2 * side + 8, width), jnp.float32),
        ],
        cost_estimate=pl.CostEstimate(
            flops=6 * blocks * side * entries * width,
            bytes_accessed=2 * blocks * side * entries,
            transcendentals=blocks * side * entries,
        ),
    )(slot, b_block, c_block, held, values, a_slots, b_panel, factor_c.reshape(-1, side, width))
    got_b = lax.all_to_all(out_b, "grid", 0, 0)
    grad_b = jnp.sum(got_b, axis=0)
    tail = grad_b[2 * side :]
    sums = jnp.stack([jnp.sum(tail[:, :128]), jnp.sum(tail[:, 128:])])
    spread = jnp.broadcast_to(jnp.repeat(sums, 64)[None, None, :], (wide_count, 1, 128))
    every = jnp.sum(lax.all_to_all(spread, "wide", 0, 0)[:, 0, :], axis=0)
    held_loss = every[0] / (every[64] * (side * side * side))
    got_a = lax.all_to_all(out_a, "wide", 0, 0)
    first_sum = jnp.sum(jnp.where(second, 0.0, got_a), axis=0)
    second_sum = jnp.sum(jnp.where(second, got_a, 0.0), axis=0)
    grad_a = jnp.concatenate([first_sum, second_sum], axis=0)
    next_a = factor_a.astype(jnp.float32) - step_size * grad_a
    next_b = factor_b.astype(jnp.float32) - step_size * grad_b[: 2 * side]
    return (next_a, next_b, held_loss)


def solution(mesh):
    in_specs = (
        P(("grid", "wide"), None, None),
        P(("grid", "wide")),
        P(("grid", "wide")),
        P(("grid", "wide")),
        P(("grid", "wide")),
        P(("grid", "wide"), None),
        P(("wide", "grid"), None),
        P(),
    )
    out_specs = (P(("grid", "wide"), None), P(("wide", "grid"), None), P())
    return jax.shard_map(
        per_device, mesh=mesh, in_specs=in_specs, out_specs=out_specs, check_vma=False
    )
```
